32 devices in a mesh: groups: 1, ep: 16 (over z, y, x), tp: 2 (over core).
Axes of the slice: x: 2, y: 2, z: 4, core: 2. Of those that a mesh axis runs over, the one named last changes fastest.
Arguments:
- tokens: bfloat16 [1024, 4096], P(('groups', 'ep'), 'tp'), may hold values from -6 to 6
- w_down: bfloat16 [4096, 1024], P('tp', 'ep'), may hold values from -0.09375 to 0.09375
- w_in: bfloat16 [16, 1024, 1344], P('ep', None, 'tp'), may hold values from -0.1875 to 0.1875
- w_out: bfloat16 [16, 1344, 1024], P('ep', 'tp'), may hold values from -0.125 to 0.125
- w_up: bfloat16 [1024, 4096], P('ep', 'tp'), may hold values from -0.1875 to 0.1875
- expert_ids: int32 [1024, 3], P(('groups', 'ep')), may hold values from 0 to 7, all different within a row; in each aligned block of 64 rows (0 to 63, 64 to 127, ...) at most 48 rows name the same one
- route_weights: float32 [1024, 3], P(('groups', 'ep')), may hold values from 0.2 to 1
Outputs:
- layer_out: bfloat16 [1024, 4096], P(('groups', 'ep'), 'tp')
The draws below stay inside these ranges and needn't reach their ends.
Inputs may be any that keep to these rules, and one draw needn't show every extreme that they name: `expert_ids`: each row names 3 different experts. In each aligned block of 64 rows (the rows of one device) no expert is named more than 48 times, a bound that some block reaches.
All inputs are finite; a program needn't handle non-finite values.
Results may differ from the reference program's by a relative error of at most 0.009.
Values may be sent and summed in bfloat16 or wider, within the bound.
No kernel may reach another device: no remote copies, remote signals or barrier semaphores. Data moves between devices by JAX's collectives and lax.ppermute only.
A program may use at most 64 MiB of HBM per device.

```python
import math
import jax
import jax.numpy as jnp
import numpy as np
from jax import lax

D = 4096
LATENT = 1024
FF = 2688
TOP = 3
TOK_DEV = 64
EXPERTS = 8
CAP = 48
TOKENS = 1024
N_EP = 16


def block_levels(own_key, dims, pieces, low, high):
    def one(dim, parts):
        draws = jax.random.uniform(jax.random.fold_in(jax.random.fold_in(own_key, 6), dim), (parts,), jnp.float32, low / len(pieces), high / len(pieces))
        return jnp.repeat(jnp.exp(draws), dims[dim] // parts).reshape((-1,) + (1,) * (len(dims) - dim - 1))

    loudness = one(*pieces[0])
    for cut in pieces[1:]:
        loudness = loudness * one(*cut)
    return loudness


def deal_out(stream_key, own, number, rows, amount, top, most, slope):
    ranking = jax.random.permutation(stream_key, amount)
    heavy_load, usual = shares(amount, rows * top, most, slope, True), shares(amount, rows * top, most, slope, False)
    places = jnp.arange(amount)

    def named(lengths, turn):
        used = int((lengths > 0).sum())
        fixed = max(1, used // 4)
        passed = fixed + (places - fixed + turn * (used - fixed)) % max(1, amount - fixed)
        return jnp.zeros((amount,), jnp.int32).at[ranking[jnp.where(places < fixed, places, passed)]].set(jnp.asarray(lengths, jnp.int32))

    lengths = jnp.where(number % 4 == 0, named(heavy_load, number // 4), named(usual, number - number // 4 - 1))
    mixed = jax.random.permutation(jax.random.fold_in(own, 3), amount)
    giver, receiver = mixed[0:amount // 2 * 2:2], mixed[1:amount // 2 * 2:2]
    margin = jnp.minimum(lengths[giver] - 1, most - lengths[receiver]) // 2
    margin = jnp.where((giver == ranking[0]) | (receiver == ranking[0]) | (lengths[receiver] == 0), 0, jnp.maximum(margin, 0))
    passed = jax.random.randint(jax.random.fold_in(own, 4), (amount // 2,), 0, 1 << 20) % (margin + 1)
    lengths = lengths.at[giver].add(-passed).at[receiver].add(passed)
    members = jnp.searchsorted(jnp.cumsum(lengths), jnp.arange(rows * top), side="right").astype(jnp.int32)
    listing = members.reshape(top, rows).T
    listing = listing[jax.random.permutation(jax.random.fold_in(own, 1), rows)]
    turn = jax.random.randint(jax.random.fold_in(own, 2), (rows, 1), 0, top)
    return jnp.take_along_axis(listing, (jnp.arange(top)[None, :] + turn) % top, axis=1)


def shares(count, total, reach, slope, full):
    portions = [(1 << 20) // math.isqrt(grade ** slope) + 1 for grade in range(1, count + 1)]
    largest = reach if full else min(reach, max(-(-total // count), total * portions[0] // sum(portions)))
    least = 1 if total - largest >= count - 1 else 0
    counts, surplus = [largest] + [least] * (count - 1), total - largest - least * (count - 1)
    while surplus > 0:
        movable = [i for i in range(1, count) if counts[i] < largest] or [i for i in range(1, count) if counts[i] < reach]
        mass, left = sum([portions[i] for i in movable]), surplus
        for i in movable:
            more = min(reach - counts[i], max(1, left * portions[i] // mass), surplus)
            counts[i] = counts[i] + more
            surplus = surplus - more
    return np.array(counts)


def normal_values(own_key, shape, deviation, limit, cuts=(), kind=jnp.bfloat16):
    values = jax.random.normal(own_key, shape, jnp.float32) * deviation
    if len(cuts) > 0:
        values = block_levels(own_key, shape, cuts, -0.22, 0.18) * values
    return jnp.clip(values, min=-limit, max=limit).astype(kind)


def setup_inputs(seed: int = 0, part: int = 0) -> dict:
    arg_keys = jax.random.split(jax.random.key(seed), 8)
    own_keys = jax.random.split(jax.random.fold_in(arg_keys[7], part), 8)
    tokens = normal_values(own_keys[0], (TOKENS, D), 1.0, 6.0, ((0, 16), (1, 2)))
    w_down = normal_values(arg_keys[1], (D, LATENT), D ** -0.5, 0.09375, ((0, 2), (1, 16)))
    w_in = normal_values(arg_keys[2], (2 * EXPERTS, LATENT, FF // 2), LATENT ** -0.5, 0.1875, ((0, 16), (2, 2)))
    w_out = normal_values(arg_keys[3], (2 * EXPERTS, FF // 2, LATENT), FF ** -0.5, 0.125, ((0, 16), (1, 2)))
    w_up = normal_values(arg_keys[4], (LATENT, D), LATENT ** -0.5, 0.1875, ((0, 16), (1, 2)))
    expert_ids_keys = jax.random.split(jax.random.fold_in(own_keys[5], 1), TOKENS // TOK_DEV)
    expert_ids_turns = jax.random.permutation(jax.random.fold_in(own_keys[5], 3), TOKENS // TOK_DEV)
    expert_ids = jax.vmap(lambda own, number: deal_out(jax.random.fold_in(own_keys[5], 2), own, number, TOK_DEV, EXPERTS, TOP, CAP, 2))(expert_ids_keys, expert_ids_turns).reshape((TOKENS, TOP))
    route_weights = jnp.clip(0.2 + 0.8 * jax.random.uniform(own_keys[6], (TOKENS, TOP), jnp.float32) ** block_levels(own_keys[6], (TOKENS, TOP), ((0, 16),), -0.2, 0.2), 0.2, 1.0)
    return {"tokens": tokens, "w_down": w_down, "w_in": w_in, "w_out": w_out, "w_up": w_up, "expert_ids": expert_ids, "route_weights": route_weights}


def reference(tokens, w_down, w_in, w_out, w_up, expert_ids, route_weights):
    latent = jnp.dot(tokens, w_down, preferred_element_type=jnp.float32).astype(jnp.bfloat16)
    pairs = TOK_DEV * TOP
    blocks = expert_ids.reshape(N_EP, pairs)
    onehot = (blocks[:, :, None] == jnp.arange(EXPERTS, dtype=jnp.int32)[None, None, :]).astype(jnp.int32)
    before = jnp.cumsum(onehot, axis=1) - onehot
    position = jnp.sum(before * onehot, axis=2).astype(jnp.int32)
    source = jnp.broadcast_to(jnp.arange(N_EP, dtype=jnp.int32)[:, None], (N_EP, pairs))
    owner = source * TOK_DEV + jnp.broadcast_to((jnp.arange(pairs, dtype=jnp.int32) // TOP)[None, :], (N_EP, pairs))
    table = jnp.full((EXPERTS, N_EP, CAP), TOKENS, jnp.int32).at[blocks, source, position].set(owner.astype(jnp.int32))
    weights = jnp.zeros((EXPERTS, N_EP, CAP), jnp.float32).at[blocks, source, position].set(route_weights.reshape(N_EP, pairs).astype(jnp.float32))
    quarter = FF // 4

    def expert_step(total, index):
        rows_of = table[index].reshape(N_EP * CAP)
        slot_weight = weights[index].reshape(N_EP * CAP)
        live = rows_of < TOKENS
        picked = latent[jnp.minimum(rows_of, TOKENS - 1)]
        picked = jnp.where(live[:, None], picked, jnp.zeros_like(picked))
        pair_in = lax.dynamic_slice_in_dim(w_in, (2 * index).astype(jnp.int32), 2, 0)
        pair_out = lax.dynamic_slice_in_dim(w_out, (2 * index).astype(jnp.int32), 2, 0)
        result = jnp.zeros((N_EP * CAP, LATENT), jnp.float32)
        for half in range(2):
            for core in range(2):
                win = pair_in[half][:, core * quarter:(core + 1) * quarter]
                wout = pair_out[half][core * quarter:(core + 1) * quarter, :]
                pre = jnp.maximum(jnp.dot(picked, win, preferred_element_type=jnp.float32), 0.0)
                hidden = (pre * pre).astype(jnp.bfloat16)
                result = result + jnp.dot(hidden, wout, preferred_element_type=jnp.float32)
        total = total.at[rows_of].add(slot_weight[:, None] * result, mode="drop")
        return total, None

    mixed, unused = lax.scan(expert_step, jnp.zeros((TOKENS, LATENT), jnp.float32), jnp.arange(EXPERTS, dtype=jnp.int32))
    mixed = mixed.astype(jnp.bfloat16)
    return jnp.dot(mixed, w_up, preferred_element_type=jnp.float32).astype(jnp.bfloat16)
```

```python
import math

import jax
import jax.numpy as jnp
from jax import lax
from jax.sharding import PartitionSpec as P


def swapped(value, axis, mask):
    pairs = [(source, source ^ mask) for source in range(lax.axis_size(axis))]
    return lax.ppermute(value, axis, pairs)


def reordered(blocks, place):
    step = 1
    while step < len(blocks):
        flip = (place & step) != 0
        blocks = [jnp.where(flip, blocks[i ^ step], blocks[i]) for i in range(len(blocks))]
        step *= 2
    return blocks


def dot(a, b):
    return jnp.dot(a, b, preferred_element_type=jnp.float32)


def slot_tables(expert_ids, experts, capacity):
    count, top = expert_ids.shape
    flat = expert_ids.reshape(count * top)
    onehot = (flat[:, None] == jnp.arange(experts, dtype=jnp.int32)[None, :]).astype(jnp.int32)
    before = jnp.cumsum(onehot, axis=0) - onehot
    position = jnp.sum(before * onehot, axis=1)
    place = flat * capacity + position
    sender = jnp.arange(count * top, dtype=jnp.int32) // top
    owner = jnp.full((experts * capacity,), count, jnp.int32).at[place].set(sender)
    return (place, owner)


def by_slots(tokens, w_down, w_in, w_out, w_up, expert_ids, route_weights):
    count, top = expert_ids.shape
    devices = lax.axis_size("ep")
    experts = devices // 2
    capacity = slot_count(count, top, devices)
    halfcap = capacity // 2
    partial_value = dot(tokens, lax.all_gather(w_down, "ep", axis=1, tiled=True))
    place, owner = slot_tables(expert_ids, experts, capacity)
    live = owner < count
    source_row = jnp.minimum(owner, count - 1)
    latent = lax.psum(partial_value, "tp").astype(jnp.bfloat16)
    outgoing = latent[source_row]
    outgoing = jnp.where(live[:, None], outgoing, jnp.zeros_like(outgoing))
    outgoing = outgoing.reshape(devices, halfcap, outgoing.shape[1])
    arrived = lax.all_to_all(outgoing, "ep", split_axis=0, concat_axis=0, tiled=True)
    parity = lax.axis_index("ep") % 2
    partner = swapped(arrived, "ep", 1)
    arrived = jnp.where(
        parity == 0,
        jnp.concatenate([arrived, partner], axis=1),
        jnp.concatenate([partner, arrived], axis=1),
    )
    rows = arrived.reshape(devices * capacity, arrived.shape[2])
    pre = jnp.maximum(dot(rows, w_in[0]), 0.0)
    result = dot((pre * pre).astype(jnp.bfloat16), w_out[0])
    result = result.reshape(devices, capacity, result.shape[1])
    width = result.shape[2]
    lower = result[:, :, : width // 2]
    upper = result[:, :, width // 2 :]
    mine = jnp.where(parity == 0, lower, upper)
    theirs = jnp.where(parity == 0, upper, lower)
    sending = mine + swapped(theirs.astype(jnp.bfloat16), "ep", 1).astype(theirs.dtype)
    returned = lax.all_to_all(sending, "ep", split_axis=0, concat_axis=0, tiled=True)
    summed = returned.reshape(experts, 2, capacity, width // 2)
    summed = jnp.transpose(summed, (0, 2, 1, 3)).reshape(experts * capacity, width)
    picked = summed[place] * route_weights.reshape(count * top)[:, None]
    mixed_part = jnp.sum(picked.reshape(count, top, width), axis=1)
    mixed = lax.psum(mixed_part, "tp").astype(jnp.bfloat16)
    layer_out = dot(mixed, lax.all_gather(w_up, "ep", axis=0, tiled=True))
    return layer_out.astype(jnp.bfloat16)


def slot_count(count, top, devices):
    return 2 * min(count // 2, max(1, count * top // (devices // 2)))


def every_row(tokens, w_down, w_in, w_out, w_up, expert_ids, route_weights):
    bf16 = jnp.bfloat16
    count, top = expert_ids.shape
    half = count // 2
    devices = lax.axis_size("ep")
    side = math.isqrt(devices)
    experts = devices // 2
    here = lax.axis_index("ep")
    inner, outer = here % side, here // side
    core = lax.axis_index("tp")

    def inner_swap(value, k):
        return swapped(value, "ep", k) if k else value

    def outer_swap(value, k):
        return swapped(value, "ep", k * side) if k else value

    def core_swap(value):
        return swapped(value, "tp", 1)

    def my_half(value):
        low, high = value[:, :half], value[:, half:]
        return (jnp.where(core == 0, low, high), jnp.where(core == 0, high, low))

    tok = [outer_swap(tokens, k) for k in range(side)]
    wd = [inner_swap(w_down.T, k) for k in range(side)]
    wd = jnp.concatenate(reordered(wd, inner), axis=0)
    partial_value = jnp.stack([dot(t, wd.T) for t in tok])
    keep, give = my_half(partial_value)
    latent = (keep + core_swap(give)).astype(bf16)

    picks = jnp.arange(experts, dtype=jnp.int32)[:, None, None] == expert_ids.T[None]
    table = jnp.sum(jnp.where(picks, route_weights.T[None], 0.0), axis=1)
    table = jnp.concatenate([outer_swap(table, k) for k in range(side)], axis=1)
    table = jnp.stack([inner_swap(table, k) for k in range(side)])
    table = lax.dynamic_index_in_dim(table, here // 2, 1, keepdims=False)
    weight_mine, weight_other = my_half(table.reshape(side * side, count))
    weight_mine = weight_mine.reshape(side, side * half, 1)
    weight_other = weight_other.reshape(side, side * half, 1)

    got = [outer_swap(latent, k) for k in range(side)]
    rows = [jnp.concatenate([got[k][m ^ k] for k in range(side)], axis=1) for m in range(side)]
    rows = jnp.concatenate(rows, axis=0)
    win = w_in[0].reshape(side, w_in.shape[1] // side, w_in.shape[2])
    win = jnp.concatenate(reordered([win[k] for k in range(side)], outer), axis=0)

    def expert(x, weight):
        pre = jnp.maximum(dot(x, win), 0.0)
        return dot((pre * pre).astype(bf16), w_out[0]) * weight

    total = None
    for k in range(side):
        mine = inner_swap(rows, k)
        other = core_swap(mine)
        part = expert(
            jnp.concatenate([mine, other], axis=0),
            jnp.concatenate([weight_mine[k], weight_other[k]], axis=0),
        )
        size = side * half
        summed = part[:size] + core_swap(part[size:].astype(bf16)).astype(jnp.float32)
        back = inner_swap(summed.astype(bf16), k).astype(jnp.float32) if k else summed
        total = back if total is None else total + back
    total = total.astype(bf16).reshape(side, half, total.shape[1])
    mixed = sum(outer_swap(total[k], k).astype(jnp.float32) for k in range(side)).astype(bf16)

    share = w_up.shape[1] // side
    up = reordered([w_up[:, k * share : (k + 1) * share] for k in range(side)], inner)
    up = jnp.concatenate(reordered([inner_swap(up[k], k) for k in range(side)], inner), axis=0)
    up = jnp.concatenate(reordered([outer_swap(up, k) for k in range(side)], outer), axis=0)
    mixed = jnp.stack([inner_swap(mixed, k) for k in range(side)])
    other = core_swap(mixed)
    low = jnp.where(core == 0, mixed, other)
    high = jnp.where(core == 0, other, mixed)
    mixed = jnp.concatenate([low, high], axis=1).reshape(side * count, low.shape[2])
    out = dot(mixed, up).astype(bf16).reshape(side, count, share)
    out = reordered([inner_swap(out[k], k) for k in range(side)], inner)
    return jnp.concatenate(out, axis=1)


def per_device(tokens, w_down, w_in, w_out, w_up, expert_ids, route_weights):
    count, top = expert_ids.shape
    devices = lax.axis_size("ep")
    side = math.isqrt(devices)
    few = count <= 2 * slot_count(count, top, devices)
    even = side * side == devices and side & (side - 1) == 0 and count % 2 == 0
    plan = every_row if few and even else by_slots
    return plan(tokens, w_down, w_in, w_out, w_up, expert_ids, route_weights)


def solution(mesh):
    in_specs = (
        P(("groups", "ep"), "tp"),
        P("tp", "ep"),
        P("ep", None, "tp"),
        P("ep", "tp", None),
        P("ep", "tp"),
        P(("groups", "ep"), None),
        P(("groups", "ep"), None),
    )
    out_specs = P(("groups", "ep"), "tp")
    return jax.shard_map(
        per_device, mesh=mesh, in_specs=in_specs, out_specs=out_specs, check_vma=False
    )
```
